32 devices in a mesh: dp: 8 (over y, x, core), mp: 4 (over z).
Axes of the slice: x: 2, y: 2, z: 4, core: 2. Of those that a mesh axis runs over, the one named last changes fastest.
Arguments:
- tokens: bfloat16 [16384, 768], P('dp'), may hold values from -6 to 6
- cotangent: bfloat16 [16384, 768], P('dp'), may hold values from -6 to 6
- random_blocks: int32 [16, 12, 14, 3], P('dp', 'mp'), may hold values from 1 to 14
- query_weight: bfloat16 [768, 768], P(None, 'mp'), may hold values from -0.21875 to 0.21875
- query_bias: bfloat16 [768], P('mp'), may hold values from -3 to 3
- key_weight: bfloat16 [768, 768], P(None, 'mp'), may hold values from -0.21875 to 0.21875
- value_weight: bfloat16 [768, 768], P(None, 'mp'), may hold values from -0.21875 to 0.21875
- value_bias: bfloat16 [768], P('mp'), may hold values from -0.59765625 to 0.59765625
- out_weight: bfloat16 [768, 768], P('mp'), may hold values from -1.75 to 1.75
- out_bias: bfloat16 [768], replicated, may hold values from -2 to 2
- attn_gain: bfloat16 [768], replicated, may hold values from 0.099609375 to 1.8984375
- attn_shift: bfloat16 [768], replicated, may hold values from -2 to 2
- up_weight: bfloat16 [768, 3072], P(None, 'mp'), may hold values from -0.21875 to 0.21875
- up_bias: bfloat16 [3072], P('mp'), may hold values from -3 to 3
- down_weight: bfloat16 [3072, 768], P('mp'), may hold values from -0.21875 to 0.21875
- down_bias: bfloat16 [768], replicated, may hold values from -2 to 2
- mlp_gain: bfloat16 [768], replicated, may hold values from 0.099609375 to 1.8984375
- mlp_shift: bfloat16 [768], replicated, may hold values from -2 to 2
Outputs:
- layer_out: float32 [16384, 768], P('dp')
- tokens_grad: float32 [16384, 768], P('dp')
- grad_query_weight: float32 [768, 768], P(None, 'mp')
- grad_query_bias: float32 [768], P('mp')
- grad_key_weight: float32 [768, 768], P(None, 'mp')
- grad_value_weight: float32 [768, 768], P(None, 'mp')
- grad_value_bias: float32 [768], P('mp')
- grad_out_weight: float32 [768, 768], P('mp')
- grad_out_bias: float32 [768], replicated
- grad_attn_gain: float32 [768], replicated
- grad_attn_shift: float32 [768], replicated
- grad_up_weight: float32 [768, 3072], P(None, 'mp')
- grad_up_bias: float32 [3072], P('mp')
- grad_down_weight: float32 [3072, 768], P('mp')
- grad_down_bias: float32 [768], replicated
- grad_mlp_gain: float32 [768], replicated
- grad_mlp_shift: float32 [768], replicated
The draws below stay inside these ranges and needn't reach their ends.
All inputs are finite; a program needn't handle non-finite values.
Results may differ from the reference program's by a relative error of at most 0.014.
The reference program's roundings to bfloat16 on the way count: a program that leaves them out, or rounds other values in their place, can miss the bound.
Values sent between devices are 32-bit elements; how exact they have to be, the bound alone decides.
A program may use at most 256 MiB of HBM per device.

```python
import math
import jax
import jax.numpy as jnp
from jax import lax

D = 768
HEADS = 12
HEAD_DIM = 64
FF = 3072
BLOCK = 64
RAND = 3
LEN = 1024
SEQS = 16
TOKENS = 16384


def touch_ends(values, rng, smallest, top_value):
    shape = values.shape
    spot = [jax.random.randint(jax.random.fold_in(rng, axis), (), 0, shape[axis]) for axis in range(len(shape))]
    values = values.at[tuple(spot)].set(smallest)
    longest = shape.index(max(shape))
    spot[longest] = (spot[longest] + 1) % shape[longest]
    return values.at[tuple(spot)].set(top_value)


def block_scale(own_key, dims, cuts, low, largest):
    loudness = 1.0
    for dim, blocks in cuts:
        heights = jax.random.uniform(jax.random.fold_in(jax.random.fold_in(own_key, 6), dim), (blocks,), jnp.float32, low / len(cuts), largest / len(cuts))
        loudness = loudness * jnp.repeat(jnp.exp(heights), dims[dim] // blocks).reshape((-1,) + (1,) * (len(dims) - 1 - dim))
    return loudness


def bell_draw(own_key, shape, spread, reach, split=(), kind=jnp.bfloat16):
    array = jax.random.normal(own_key, shape, jnp.float32) * spread
    if len(split) > 0:
        array = block_scale(own_key, shape, split, -0.22, 0.18) * array
    return jnp.clip(array, min=-reach, max=reach).astype(kind)


def setup_inputs(seed: int = 0) -> dict:
    key_of = jax.random.split(jax.random.key(seed), 19)
    tokens = bell_draw(key_of[0], (TOKENS, D), 1.0, 6.0, ((0, 8),))
    cotangent = bell_draw(key_of[1], (TOKENS, D), 1.0, 6.0, ((0, 8),))
    random_blocks = touch_ends(jax.random.randint(key_of[2], (SEQS, HEADS, LEN // BLOCK - 2, RAND), 1, LEN // BLOCK - 1), jax.random.fold_in(key_of[2], 1), 1, (LEN // BLOCK - 1) - 1).astype(jnp.int32)
    query_weight = bell_draw(key_of[3], (D, D), D ** -0.5, 0.21875, ((1, 4),))
    query_bias = bell_draw(key_of[4], (D,), 0.5, 3.0, ((0, 4),))
    key_weight = bell_draw(key_of[5], (D, D), D ** -0.5, 0.21875, ((1, 4),))
    value_weight = bell_draw(key_of[6], (D, D), D ** -0.5, 0.21875, ((1, 4),))
    value_bias = bell_draw(key_of[7], (D,), 0.1, 0.59765625, ((0, 4),))
    out_weight = bell_draw(key_of[8], (D, D), (D // 64) ** -0.5, 1.75, ((0, 4),))
    out_bias = bell_draw(key_of[9], (D,), 0.3, 2.0)
    attn_gain = jnp.clip(1.0 + 0.18 * jax.random.normal(key_of[10], (D,), jnp.float32), 0.099609375, 1.8984375).astype(jnp.bfloat16)
    attn_shift = bell_draw(key_of[11], (D,), 0.3, 2.0)
    up_weight = bell_draw(key_of[12], (D, FF), D ** -0.5, 0.21875, ((1, 4),))
    up_bias = bell_draw(key_of[13], (FF,), 0.5, 3.0, ((0, 4),))
    down_weight = bell_draw(key_of[14], (FF, D), (FF // 4) ** -0.5, 0.21875, ((0, 4),))
    down_bias = bell_draw(key_of[15], (D,), 0.3, 2.0)
    mlp_gain = jnp.clip(1.0 + 0.18 * jax.random.normal(key_of[16], (D,), jnp.float32), 0.099609375, 1.8984375).astype(jnp.bfloat16)
    mlp_shift = bell_draw(key_of[17], (D,), 0.3, 2.0)
    return {"tokens": tokens, "cotangent": cotangent, "random_blocks": random_blocks, "query_weight": query_weight, "query_bias": query_bias, "key_weight": key_weight, "value_weight": value_weight, "value_bias": value_bias, "out_weight": out_weight, "out_bias": out_bias, "attn_gain": attn_gain, "attn_shift": attn_shift, "up_weight": up_weight, "up_bias": up_bias, "down_weight": down_weight, "down_bias": down_bias, "mlp_gain": mlp_gain, "mlp_shift": mlp_shift}


@jax.custom_vjp
def low(v):
    return lax.optimization_barrier(v.astype(jnp.bfloat16)).astype(jnp.float32)

@jax.custom_vjp
def low_back(v):
    return v

def low_keep(v):
    return (low(v), None)

def low_pass(kept, grad):
    return (grad,)

def back_keep(v):
    return (v, None)

def back_low(kept, grad):
    return (low(grad),)
low.defvjp(low_keep, low_pass)
low_back.defvjp(back_keep, back_low)
EPSILON = 1e-05
HIGHEST = lax.Precision.HIGHEST

def norm_rows(summed, scale_gain, shift):
    row_mean = lax.optimization_barrier(jnp.mean(summed, -1, keepdims=True))
    centered = summed - row_mean
    variance = lax.optimization_barrier(jnp.mean(centered * centered, -1, keepdims=True))
    return centered * lax.rsqrt(variance + EPSILON) * scale_gain + shift

def head_attend(queries, key_rows, value_rows, chosen):
    block_count = LEN // BLOCK
    q_blocks = queries.reshape(block_count, BLOCK, -1)
    k_blocks = key_rows.reshape(block_count, BLOCK, -1)
    v_blocks = value_rows.reshape(block_count, BLOCK, -1)
    middle = jnp.arange(1, block_count - 1, dtype=jnp.int32)
    fixed = jnp.stack([middle - 1, middle, middle + 1, jnp.zeros_like(middle), jnp.full_like(middle, block_count - 1)], 1)
    listed = jnp.concatenate([fixed, chosen.astype(jnp.int32)], 1)
    k_listed = k_blocks[listed].reshape(block_count - 2, (5 + RAND) * BLOCK, -1)
    v_listed = v_blocks[listed].reshape(block_count - 2, (5 + RAND) * BLOCK, -1)
    scores = low_back(jnp.einsum('mqd,mkd->mqk', q_blocks[1:block_count - 1], k_listed, precision=HIGHEST) * 0.125)
    soft = low(jax.nn.softmax(scores, axis=-1))
    out_middle = jnp.einsum('mqk,mkd->mqd', soft, v_listed, precision=HIGHEST)
    q_global = jnp.stack([q_blocks[0], q_blocks[block_count - 1]], 0)
    scores_global = low_back(jnp.einsum('gqd,kd->gqk', q_global, key_rows, precision=HIGHEST) * 0.125)
    soft_global = low(jax.nn.softmax(scores_global, axis=-1))
    out_global = jnp.einsum('gqk,kd->gqd', soft_global, value_rows, precision=HIGHEST)
    return jnp.concatenate([out_global[0:1], out_middle, out_global[1:2]], 0).reshape(LEN, -1)

def layer(inputs, params, tables):
    query_weight, query_bias, key_weight, value_weight, value_bias, out_weight, out_bias, attn_gain, attn_shift, up_weight, up_bias, down_weight, down_bias, mlp_gain, mlp_shift = params
    group = inputs.shape[0] // LEN
    queries = low_back(low(jnp.dot(inputs, query_weight, precision=HIGHEST) + query_bias))
    key_rows = low_back(low(jnp.dot(inputs, key_weight, precision=HIGHEST)))
    value_rows = low_back(low(jnp.dot(inputs, value_weight, precision=HIGHEST) + value_bias))

    def split_heads(flat):
        return flat.reshape(group, LEN, HEADS, HEAD_DIM).transpose(0, 2, 1, 3)
    attended = jax.vmap(jax.vmap(head_attend))(split_heads(queries), split_heads(key_rows), split_heads(value_rows), tables)
    attended = low_back(low(attended.transpose(0, 2, 1, 3).reshape(group * LEN, D)))
    attn_branch = low_back(jnp.dot(attended, out_weight, precision=HIGHEST) + out_bias)
    hidden = norm_rows(inputs + attn_branch, attn_gain, attn_shift)
    hidden_low = low(hidden)
    up_value = low_back(jnp.dot(hidden_low, up_weight, precision=HIGHEST) + up_bias)
    active = low(jax.nn.gelu(up_value, approximate=True))
    mlp_branch = low_back(jnp.dot(active, down_weight, precision=HIGHEST) + down_bias)
    return norm_rows(hidden + mlp_branch, mlp_gain, mlp_shift)

def reference(tokens, cotangent, random_blocks, query_weight, query_bias, key_weight, value_weight, value_bias, out_weight, out_bias, attn_gain, attn_shift, up_weight, up_bias, down_weight, down_bias, mlp_gain, mlp_shift):
    params = tuple((a.astype(jnp.float32) for a in (query_weight, query_bias, key_weight, value_weight, value_bias, out_weight, out_bias, attn_gain, attn_shift, up_weight, up_bias, down_weight, down_bias, mlp_gain, mlp_shift)))
    group = math.gcd(SEQS, max(1, 4096 // LEN))
    turns = SEQS // group
    inputs = tokens.astype(jnp.float32).reshape(turns, group * LEN, D)
    grads_in = cotangent.astype(jnp.float32).reshape(turns, group * LEN, D)
    tables = random_blocks.reshape(turns, group, HEADS, LEN // BLOCK - 2, RAND)

    def one_group(summed, item):
        inputs_now, grad_now, table_now = item
        result, pull = jax.vjp(lambda xx, pp: layer(xx, pp, table_now), inputs_now, params)
        grad_inputs, grad_params = pull(grad_now)
        return (tuple((a + b for a, b in zip(summed, grad_params))), (result, grad_inputs))
    zeros = tuple((jnp.zeros_like(p) for p in params))
    summed, (results, grad_inputs) = lax.scan(one_group, zeros, (inputs, grads_in, tables))
    return (results.reshape(TOKENS, D), grad_inputs.reshape(TOKENS, D), summed[0], summed[1], summed[2], summed[3], summed[4], summed[5], summed[6], summed[7], summed[8], summed[9], summed[10], summed[11], summed[12], summed[13], summed[14])
```

```python
import functools

import jax
import jax.numpy as jnp
from jax import lax
from jax.experimental import pallas as pl
from jax.experimental.pallas import tpu as pltpu
from jax.sharding import PartitionSpec as P

D = 768
HEAD_DIM = 64
BLOCK = 64
LEN = 1024
NB = LEN // BLOCK
RAND = 3
LISTED = 5 + RAND
GROUP = 4
GW = GROUP * HEAD_DIM
EPSILON = 1e-05
SCALING = 0.125
PIECES = 8
PR = D // PIECES
TILE = 256
F32 = jnp.float32
BF16 = jnp.bfloat16
VMEM_LIMIT = 60 * 1024 * 1024
SQRT_2_PI = 0.7978845608028654
CUBIC = 0.044715


def dot_nn(a, b):
    return lax.dot_general(a, b, (((1,), (0,)), ((), ())), preferred_element_type=F32)


def dot_nt(a, b):
    return lax.dot_general(a, b, (((1,), (1,)), ((), ())), preferred_element_type=F32)


def dot_tn(a, b):
    return lax.dot_general(a, b, (((0,), (0,)), ((), ())), preferred_element_type=F32)


def params(**kw):
    return pltpu.CompilerParams(vmem_limit_bytes=VMEM_LIMIT, **kw)


def cost(flops, nbytes):
    return pl.CostEstimate(flops=int(flops), bytes_accessed=int(nbytes), transcendentals=0)


def vmem():
    return pl.BlockSpec(memory_space=pltpu.VMEM)


def swap(x, axis, size, bit):
    return lax.ppermute(x, axis, [(i, i ^ bit) for i in range(size)])


def gather_line(piece, mp):
    first = swap(piece, "mp", mp, 1)
    second = swap(piece, "mp", mp, 2)
    third = swap(second, "mp", mp, 1)
    return jnp.stack([first, second, third], 0)


def gather_plane(own, dp):
    half = own.shape[-2] // 2
    core = swap(own, "dp", dp, 1)
    xs = swap(own, "dp", dp, 2)
    ys = swap(own, "dp", dp, 4)
    low = swap(xs[..., :half, :], "dp", dp, 4)
    high = swap(ys[..., half:, :], "dp", dp, 2)
    return (
        own,
        core,
        xs,
        swap(xs, "dp", dp, 1),
        ys,
        swap(ys, "dp", dp, 1),
        low,
        high,
        swap(low, "dp", dp, 1),
        swap(high, "dp", dp, 1),
    )


def each_piece(refs, rows):
    half = rows // 2
    for u in range(6):
        yield u, 0, rows, refs[u]
    yield 6, 0, half, refs[6]
    yield 6, half, half, refs[7]
    yield 7, 0, half, refs[8]
    yield 7, half, half, refs[9]


def place_attn(sc, own, *refs):
    out = refs[-1]
    rank, spot = sc[0], sc[1]
    width = D // 4
    for k in range(4):
        at = pl.multiple_of(spot * width, 64)
        out[k, pl.ds(at, width), :] = own[k * width : (k + 1) * width, :]
    for u, start, rows, ref in each_piece(refs[:-1], PR):
        where = lax.bitwise_xor(u, rank)
        kind = lax.shift_right_logical(where, 1)
        base = lax.bitwise_and(where, 1) * PR + start
        for t in range(3):
            at = pl.multiple_of(lax.bitwise_xor(spot, t + 1) * width + base, 16)
            out[kind, pl.ds(at, rows), :] = ref[t].astype(BF16)


def place_mlp(sc, own_up, own_down, *refs):
    up, down = refs[-2:]
    rank, spot = sc[0], sc[1]
    at = pl.multiple_of(spot * D, 256)
    up[pl.ds(at, D), :] = own_up[...]
    down[pl.ds(at, D), :] = own_down[...]
    for n, out in enumerate((up, down)):
        for u, ref in enumerate(refs[10 * n : 10 * n + 10]):
            pass
        for u, start, rows, ref in each_piece(refs[10 * n : 10 * n + 10], PR):
            base = lax.bitwise_xor(u, rank) * PR + start
            for t in range(3):
                at = pl.multiple_of(lax.bitwise_xor(spot, t + 1) * D + base, 16)
                out[pl.ds(at, rows), :] = ref[t].astype(BF16)


def call_place(body, sc, operands, out_shapes):
    total = sum(a.size * a.dtype.itemsize for a in operands)
    return pl.pallas_call(
        body,
        out_shape=out_shapes,
        in_specs=[pl.BlockSpec(memory_space=pltpu.SMEM)] + [vmem()] * len(operands),
        out_specs=jax.tree.map(lambda _: vmem(), out_shapes),
        compiler_params=params(),
        cost_estimate=cost(0, 2 * total),
    )(sc, *operands)


def lane_masks(rows):
    lane = lax.broadcasted_iota(jnp.int32, (rows, GW), 1)
    return [(lane // HEAD_DIM == h) for h in range(GROUP)]


def spread_heads(block, masks):
    zero = jnp.zeros_like(block)
    return jnp.concatenate([jnp.where(m, block, zero) for m in masks], 0)


def fold_heads(wide, masks):
    out = jnp.zeros((BLOCK, GW), F32)
    for h in range(GROUP):
        out = jnp.where(masks[h], wide[h * BLOCK : (h + 1) * BLOCK, :], out)
    return out


def listed_at(table, group, b, i):
    return [
        table[((group * GROUP + h) * (NB - 2) + b - 1) * RAND + i] * BLOCK for h in range(GROUP)
    ]


def list_rows(ref, table, group, b, masks):
    near = ref[pl.ds(pl.multiple_of((b - 1) * BLOCK, BLOCK), 3 * BLOCK), :]
    parts = [near, ref[0:BLOCK, :], ref[LEN - BLOCK : LEN, :]]
    for i in range(RAND):
        at = listed_at(table, group, b, i)
        picked = ref[pl.ds(pl.multiple_of(at[0], BLOCK), BLOCK), :]
        for h in range(1, GROUP):
            picked = jnp.where(
                masks[h], ref[pl.ds(pl.multiple_of(at[h], BLOCK), BLOCK), :], picked
            )
        parts.append(picked)
    return jnp.concatenate(parts, 0)


def attend_block(query, keys, values, masks):
    scores = dot_nt(keys, spread_heads(query, masks)) * SCALING
    highest = jnp.max(scores, 0, keepdims=True)
    raised = jnp.exp(scores - highest)
    total = jnp.sum(raised, 0, keepdims=True)
    soft = (raised * (1.0 / total)).astype(BF16)
    return fold_heads(dot_tn(soft, values), masks).astype(BF16), highest + jnp.log(total)


def attn_fwd(sc, table, x, wq, wk, wv, qb, vb, q, k, v, att, lse):
    group = pl.program_id(0)
    rows = x[...]
    q[...] = (dot_nt(rows, wq[0]) + qb[...]).astype(BF16)
    k[...] = dot_nt(rows, wk[0]).astype(BF16)
    v[...] = (dot_nt(rows, wv[0]) + vb[...]).astype(BF16)
    masks = lane_masks(BLOCK)

    @pl.loop(0, 2)
    def _(n):
        b = n * (NB - 1)
        at = pl.ds(pl.multiple_of(b * BLOCK, BLOCK), BLOCK)
        out, logsum = attend_block(q[at, :], k[...], v[...], masks)
        att[at, :] = out
        lse[0, pl.ds(b, 1), :] = logsum

    @pl.loop(1, NB - 1)
    def _(b):
        at = pl.ds(pl.multiple_of(b * BLOCK, BLOCK), BLOCK)
        keys = list_rows(k, table, group, b, masks)
        values = list_rows(v, table, group, b, masks)
        out, logsum = attend_block(q[at, :], keys, values, masks)
        att[at, :] = out
        lse[0, pl.ds(b, 1), :] = logsum


def call_attn_fwd(sc, table, tokens, w4, qb, vb):
    groups = D // GW
    wspec = lambda n: pl.BlockSpec((1, GW, D), lambda g, *_: (n, g, 0))
    col = pl.BlockSpec((LEN, GW), lambda g, *_: (0, g))
    row = pl.BlockSpec((1, GW), lambda g, *_: (0, g))
    flat = jax.ShapeDtypeStruct((LEN, D), BF16)
    return pl.pallas_call(
        attn_fwd,
        out_shape=(flat, flat, flat, flat, jax.ShapeDtypeStruct((groups, NB, GW), F32)),
        grid_spec=pltpu.PrefetchScalarGridSpec(
            num_scalar_prefetch=2,
            grid=(groups,),
            in_specs=[
                pl.BlockSpec((LEN, D), lambda g, s, *_: (s[2], 0)),
                wspec(0),
                wspec(1),
                wspec(2),
                row,
                row,
            ],
            out_specs=(col, col, col, col, pl.BlockSpec((1, NB, GW), lambda g, *_: (g, 0, 0))),
        ),
        compiler_params=params(),
        cost_estimate=cost(3e10, 2e7),
    )(sc, table, tokens, w4, w4, w4, qb, vb)


def back_block(query, keys, values, grad_out, logsum, masks):
    wide_q = spread_heads(query, masks)
    wide_g = spread_heads(grad_out, masks)
    soft = jnp.exp(dot_nt(keys, wide_q) * SCALING - logsum)
    grad_soft = dot_nt(values, wide_g)
    inner = jnp.sum(soft * grad_soft, 0, keepdims=True)
    grad_scores = (soft * (grad_soft - inner)).astype(BF16)
    grad_q = fold_heads(dot_tn(grad_scores, keys), masks) * SCALING
    grad_k = dot_nn(grad_scores, wide_q)
    grad_v = dot_nn(soft.astype(BF16), wide_g)
    return grad_q.astype(BF16), grad_k, grad_v


def attn_back(sc, table, q, k, v, go, lse, dq, dk, dv, sums, acc_k, acc_v):
    group = pl.program_id(0)
    masks = lane_masks(BLOCK)
    acc_k[...] = jnp.zeros_like(acc_k)
    acc_v[...] = jnp.zeros_like(acc_v)

    @pl.loop(0, 2)
    def _(n):
        b = n * (NB - 1)
        at = pl.ds(pl.multiple_of(b * BLOCK, BLOCK), BLOCK)
        gq, gk, gv = back_block(
            q[at, :], k[...], v[...], go[at, :], lse[0, pl.ds(b, 1), :], masks
        )
        dq[at, :] = gq
        acc_k[...] += gk
        acc_v[...] += gv

    @pl.loop(1, NB - 1)
    def _(b):
        at = pl.ds(pl.multiple_of(b * BLOCK, BLOCK), BLOCK)
        keys = list_rows(k, table, group, b, masks)
        values = list_rows(v, table, group, b, masks)
        gq, gk, gv = back_block(q[at, :], keys, values, go[at, :], lse[0, pl.ds(b, 1), :], masks)
        dq[at, :] = gq
        near = pl.ds(pl.multiple_of((b - 1) * BLOCK, BLOCK), 3 * BLOCK)
        zero = jnp.zeros((BLOCK, GW), F32)
        for acc, listed in ((acc_k, gk), (acc_v, gv)):
            acc[near, :] += listed[0 : 3 * BLOCK, :]
            acc[0:BLOCK, :] += listed[3 * BLOCK : 4 * BLOCK, :]
            acc[LEN - BLOCK : LEN, :] += listed[4 * BLOCK : 5 * BLOCK, :]
            for i in range(RAND):
                part = listed[(5 + i) * BLOCK : (6 + i) * BLOCK, :]
                at_heads = listed_at(table, group, b, i)
                for h in range(GROUP):
                    there = pl.ds(pl.multiple_of(at_heads[h], BLOCK), BLOCK)
                    c = (h // 2) * 128
                    acc[there, c : c + 128] += jnp.where(masks[h], part, zero)[:, c : c + 128]

    dk[...] = (acc_k[...] * SCALING).astype(BF16)
    dv[...] = acc_v[...].astype(BF16)
    sums[...] = jnp.zeros_like(sums)
    sums[0:1, :] = jnp.sum(dq[...].astype(F32), 0, keepdims=True)
    sums[1:2, :] = jnp.sum(dv[...].astype(F32), 0, keepdims=True)


def call_attn_back(sc, table, q, k, v, go, lse):
    groups = D // GW
    col = pl.BlockSpec((LEN, GW), lambda g, *_: (0, g))
    flat = jax.ShapeDtypeStruct((LEN, D), BF16)
    return pl.pallas_call(
        attn_back,
        out_shape=(flat, flat, flat, jax.ShapeDtypeStruct((8, D), F32)),
        grid_spec=pltpu.PrefetchScalarGridSpec(
            num_scalar_prefetch=2,
            grid=(groups,),
            in_specs=[col, col, col, col, pl.BlockSpec((1, NB, GW), lambda g, *_: (g, 0, 0))],
            out_specs=(col, col, col, pl.BlockSpec((8, GW), lambda g, *_: (0, g))),
            scratch_shapes=[pltpu.VMEM((LEN, GW), F32), pltpu.VMEM((LEN, GW), F32)],
        ),
        compiler_params=params(),
        cost_estimate=cost(5e10, 2e7),
    )(sc, table, q, k, v, go, lse)


def norm_stats(summed):
    row_mean = jnp.mean(summed, -1, keepdims=True)
    centered = summed - row_mean
    scaling = lax.rsqrt(jnp.mean(centered * centered, -1, keepdims=True) + EPSILON)
    return centered * scaling, scaling


def norm_back(grad_result, normed, scaling, scale_gain):
    grad_normed = grad_result * scale_gain
    inner_mean = jnp.mean(grad_normed, -1, keepdims=True)
    cross_mean = jnp.mean(grad_normed * normed, -1, keepdims=True)
    return scaling * (grad_normed - inner_mean - normed * cross_mean)


def column_sum(values):
    return jnp.sum(values.astype(F32), 0, keepdims=True)


def middle(
    sc, att, tok, cot, wo, up, down, vecs, up_bias,
    lay_own, lay_all, act, gup, hid, gml, gai, gal, gatt, sums, usum,
    act_scr, slope_scr,
):
    half = sc[3]
    first = pl.program_id(0) == 0
    out_bias, gain_one, shift_one = vecs[0:1, :], vecs[1:2, :], vecs[2:3, :]
    down_bias, gain_two, shift_two = vecs[3:4, :], vecs[4:5, :], vecs[5:6, :]
    branch = dot_nn(att[...], wo[0]) + out_bias
    normed_attn, scale_attn = norm_stats(tok[...].astype(F32) + branch)
    hidden = normed_attn * gain_one + shift_one
    hidden_low = hidden.astype(BF16)
    hid[...] = hidden_low
    mlp = jnp.zeros((TILE, D), F32)
    for n in range(4):
        at = slice(n * D, (n + 1) * D)
        u = dot_nt(hidden_low, up[at, :]) + up_bias[0:1, at]
        square = u * u
        bend = jnp.tanh(SQRT_2_PI * (u + CUBIC * (square * u)))
        active = (0.5 * u * (1.0 + bend)).astype(BF16)
        slope_scr[:, at] = 0.5 * (1.0 + bend) + (0.5 * u) * (1.0 - bend * bend) * (
            SQRT_2_PI * (1.0 + 3.0 * CUBIC * square)
        )
        act_scr[:, at] = active
        mlp = mlp + dot_nn(active, down[at, :])
    normed_mlp, scale_mlp = norm_stats(hidden + (mlp + down_bias))
    result = normed_mlp * gain_two + shift_two
    lay_own[...] = result
    lay_all[...] = result
    grad_result = cot[...].astype(F32)
    grad_mlp_in = norm_back(grad_result, normed_mlp, scale_mlp, gain_two)
    grad_mlp_low = grad_mlp_in.astype(BF16)
    gml[...] = grad_mlp_low
    back = jnp.zeros((TILE, D), F32)

    @pl.when(first)
    def _():
        sums[...] = jnp.zeros_like(sums)
        usum[...] = jnp.zeros_like(usum)

    for n in range(4):
        at = slice(n * D, (n + 1) * D)
        grad_active = dot_nt(grad_mlp_low, down[at, :])
        grad_up = (grad_active * slope_scr[:, at]).astype(BF16)
        back = back + dot_nn(grad_up, up[at, :])
        to = slice((n % 2) * D, (n % 2 + 1) * D)

        @pl.when(half == n // 2)
        def _():
            act[:, to] = act_scr[:, at]
            gup[:, to] = grad_up
            usum[0:1, to] += column_sum(grad_up)

    grad_hidden = grad_mlp_in + back
    grad_attn_in = norm_back(grad_hidden, normed_attn, scale_attn, gain_one)
    grad_attn_low = grad_attn_in.astype(BF16)
    gai[...] = grad_attn_in
    gal[...] = grad_attn_low
    gatt[...] = dot_nt(grad_attn_low, wo[0]).astype(BF16)
    sums[0:1, :] += column_sum(grad_result * normed_mlp)
    sums[1:2, :] += column_sum(grad_result)
    sums[2:3, :] += column_sum(grad_mlp_low)
    sums[3:4, :] += column_sum(grad_hidden * normed_attn)
    sums[4:5, :] += column_sum(grad_hidden)
    sums[5:6, :] += column_sum(grad_attn_low)


def call_middle(sc, att, tokens, cotangent, w4, up, down, vecs, up_bias):
    tiles = LEN // TILE
    row = lambda w: pl.BlockSpec((TILE, w), lambda i, *_: (i, 0))
    seq = pl.BlockSpec((TILE, D), lambda i, s, *_: (s[2] * tiles + i, 0))
    whole = lambda shape: pl.BlockSpec(
        shape, lambda i, *_: (0,) * len(shape), pipeline_mode=pl.Buffered(1)
    )
    sd = jax.ShapeDtypeStruct
    ff = up.shape[0]
    return pl.pallas_call(
        middle,
        out_shape=(
            sd((LEN, D), F32),
            sd((2 * LEN, D), F32),
            sd((LEN, ff // 2), BF16),
            sd((LEN, ff // 2), BF16),
            sd((LEN, D), BF16),
            sd((LEN, D), BF16),
            sd((LEN, D), F32),
            sd((LEN, D), BF16),
            sd((LEN, D), BF16),
            sd((8, D), F32),
            sd((8, ff // 2), F32),
        ),
        grid_spec=pltpu.PrefetchScalarGridSpec(
            num_scalar_prefetch=1,
            grid=(tiles,),
            in_specs=[
                row(D),
                seq,
                seq,
                pl.BlockSpec((1, D, D), lambda i, *_: (3, 0, 0), pipeline_mode=pl.Buffered(1)),
                whole((ff, D)),
                whole((ff, D)),
                whole((8, D)),
                whole((8, ff)),
            ],
            out_specs=(
                row(D),
                seq,
                row(ff // 2),
                row(ff // 2),
                row(D),
                row(D),
                row(D),
                row(D),
                row(D),
                pl.BlockSpec((8, D), lambda i, *_: (0, 0)),
                pl.BlockSpec((8, ff // 2), lambda i, *_: (0, 0)),
            ),
            scratch_shapes=[pltpu.VMEM((TILE, ff), BF16), pltpu.VMEM((TILE, ff), F32)],
        ),
        compiler_params=params(),
        cost_estimate=cost(4e10, 4e7),
    )(sc, att, tokens, cotangent, w4, up, down, vecs, up_bias)


def final_rows(sc, gai, dq, dk, dv, wq, wk, wv, own, everything):
    total = gai[...] + dot_nn(dq[...], wq[0]) + dot_nn(dk[...], wk[0]) + dot_nn(dv[...], wv[0])
    own[...] = total
    everything[...] = total


def call_final(sc, gai, dq, dk, dv, w4):
    tiles = LEN // TILE
    row = pl.BlockSpec((TILE, D), lambda i, *_: (i, 0))
    seq = pl.BlockSpec((TILE, D), lambda i, s, *_: (s[2] * tiles + i, 0))
    wspec = lambda n: pl.BlockSpec((1, D, D), lambda i, *_: (n, 0, 0))
    return pl.pallas_call(
        final_rows,
        out_shape=(
            jax.ShapeDtypeStruct((LEN, D), F32),
            jax.ShapeDtypeStruct((2 * LEN, D), F32),
        ),
        grid_spec=pltpu.PrefetchScalarGridSpec(
            num_scalar_prefetch=1,
            grid=(tiles,),
            in_specs=[row, row, row, row, wspec(0), wspec(1), wspec(2)],
            out_specs=(row, seq),
        ),
        compiler_params=params(),
        cost_estimate=cost(5e9, 2e7),
    )(sc, gai, dq, dk, dv, w4, w4, w4)


def put_rows(sc, other, everything, out):
    out[...] = other[...]


def call_put(sc, other, everything):
    tiles = LEN // TILE
    return pl.pallas_call(
        put_rows,
        out_shape=jax.ShapeDtypeStruct(everything.shape, F32),
        grid_spec=pltpu.PrefetchScalarGridSpec(
            num_scalar_prefetch=1,
            grid=(tiles,),
            in_specs=[
                pl.BlockSpec((TILE, D), lambda i, *_: (i, 0)),
                pl.BlockSpec(memory_space=pl.ANY),
            ],
            out_specs=pl.BlockSpec((TILE, D), lambda i, s, *_: ((1 - s[2]) * tiles + i, 0)),
        ),
        input_output_aliases={2: 0},
        compiler_params=params(),
        cost_estimate=cost(0, 6e6),
    )(sc, other, everything)


def split_pieces(sc, scratch, base, rows, keep, send, to):
    chip, core = lax.shift_right_logical(sc[0], 1), lax.bitwise_and(sc[0], 1)
    for c in range(4):
        there = lax.bitwise_xor(c, chip)
        mine = pl.multiple_of(base + (2 * c + core) * rows, 8)
        theirs = pl.multiple_of(base + (2 * c + 1 - core) * rows, 8)
        keep[there, to, :] = scratch[pl.ds(mine, rows), :]
        send[there, to, :] = scratch[pl.ds(theirs, rows), :]


ROWS_A = 2 * (PR + PR + PR // 4)


def weights_mid(sc, act, gml, att, gal, hid, gup0, gup1, keep, send, scr):
    small = PR // 4
    scr[0 : 2 * D, :] = dot_tn(act[...], gml[...])
    for n in range(2):
        split_pieces(sc, scr, n * D, PR, keep, send, slice(n * PR, (n + 1) * PR))
    for n, gup in enumerate((gup0, gup1)):
        scr[0:D, :] = dot_tn(hid[...], gup[...])
        split_pieces(sc, scr, 0, PR, keep, send, slice((2 + n) * PR, (3 + n) * PR))
    scr[0 : D // 2, :] = dot_tn(att[...], gal[...])
    for n in range(2):
        at = slice(4 * PR + n * small, 4 * PR + (n + 1) * small)
        split_pieces(sc, scr, n * (D // 4), small, keep, send, at)


def call_weights_mid(sc, act, gml, att, gal, hid, gup):
    width = 256
    steps = D // width
    col = pl.BlockSpec((LEN, width), lambda n, *_: (0, n))
    one = lambda w: pl.BlockSpec((LEN, w), lambda n, *_: (0, 0), pipeline_mode=pl.Buffered(1))
    out = jax.ShapeDtypeStruct((4, ROWS_A, D), F32)
    ospec = pl.BlockSpec((4, ROWS_A, width), lambda n, *_: (0, 0, n))
    return pl.pallas_call(
        weights_mid,
        out_shape=(out, out),
        grid_spec=pltpu.PrefetchScalarGridSpec(
            num_scalar_prefetch=1,
            grid=(steps,),
            in_specs=[
                one(2 * D),
                col,
                pl.BlockSpec((LEN, D // 2), lambda n, s: (0, s[3]), pipeline_mode=pl.Buffered(1)),
                col,
                one(D),
                col,
                pl.BlockSpec((LEN, width), lambda n, *_: (0, steps + n)),
            ],
            out_specs=(ospec, ospec),
            scratch_shapes=[pltpu.VMEM((2 * D, width), F32)],
        ),
        compiler_params=params(),
        cost_estimate=cost(1e10, 2e7),
    )(sc, act, gml, att, gal, hid, gup, gup)


def weights_qkv(sc, x, dq, dk, dv, keep, send, scr):
    width = D // 2
    for n, ref in enumerate((dq, dk, dv)):
        scr[...] = dot_tn(x[...], ref[...])
        chip, core = lax.shift_right_logical(sc[0], 1), lax.bitwise_and(sc[0], 1)
        cols = slice(n * width, (n + 1) * width)
        for c in range(4):
            there = lax.bitwise_xor(c, chip)
            mine = pl.multiple_of((2 * c + core) * PR, 8)
            theirs = pl.multiple_of((2 * c + 1 - core) * PR, 8)
            keep[there, :, cols] = scr[pl.ds(mine, PR), :]
            send[there, :, cols] = scr[pl.ds(theirs, PR), :]


def call_weights_qkv(sc, tokens, dq, dk, dv):
    width = D // 2
    part = pl.BlockSpec((LEN, width), lambda i, s: (0, s[3]))
    shape = (4, PR, 3 * width)
    out = jax.ShapeDtypeStruct(shape, F32)
    ospec = pl.BlockSpec(shape, lambda i, *_: (0, 0, 0))
    return pl.pallas_call(
        weights_qkv,
        out_shape=(out, out),
        grid_spec=pltpu.PrefetchScalarGridSpec(
            num_scalar_prefetch=1,
            grid=(1,),
            in_specs=[pl.BlockSpec((LEN, D), lambda i, s: (s[2], 0)), part, part, part],
            out_specs=(ospec, ospec),
            scratch_shapes=[pltpu.VMEM((D, width), F32)],
        ),
        compiler_params=params(),
        cost_estimate=cost(4e9, 1e7),
    )(sc, tokens, dq, dk, dv)


def reduce_plane(keep, send, dp):
    came = swap(send, "dp", dp, 1)
    parts = [keep[t] + came[t] for t in range(4)]
    total = parts[0]
    for t in range(1, 4):
        total = total + swap(parts[t], "dp", dp, 2 * t)
    bit = PIECES
    while bit < dp:
        total = total + swap(total, "dp", dp, bit)
        bit *= 2
    return total


def all_sum(x, dp, mp):
    bit = 1
    while bit < dp:
        x = x + swap(x, "dp", dp, bit)
        bit *= 2
    return x + swap(x, "mp", mp, 1)


def pair_sum(low, high, odd, mp):
    mine = jnp.where(odd, high, low)
    theirs = jnp.where(odd, low, high)
    return mine + swap(theirs, "mp", mp, 1)


def place_mid(sc, *refs):
    down, up, out = refs[-3:]
    rank = sc[0]
    small = PR // 4
    for u, ref in enumerate(refs[:-3]):
        where = lax.bitwise_xor(u, rank)
        at = pl.ds(pl.multiple_of(where * PR, 8), PR)
        down[at, :] = ref[0:PR, :]
        up[at, :] = ref[PR : 2 * PR, :]
        out[pl.ds(pl.multiple_of(where * small, 8), small), :] = ref[2 * PR :, :]


def place_qkv(sc, *refs):
    outs = refs[-3:]
    width = D // 4
    for u, ref in enumerate(refs[:-3]):
        where = lax.bitwise_xor(u, sc[0])
        at = pl.ds(pl.multiple_of(where * PR, 8), PR)
        for n, out in enumerate(outs):
            out[at, :] = ref[:, n * width : (n + 1) * width]


def spread_plane(own, dp):
    core = swap(own, "dp", dp, 1)
    xs = swap(own, "dp", dp, 2)
    ys = swap(own, "dp", dp, 4)
    xy = swap(xs, "dp", dp, 4)
    return (
        own,
        core,
        xs,
        swap(xs, "dp", dp, 1),
        ys,
        swap(ys, "dp", dp, 1),
        xy,
        swap(xy, "dp", dp, 1),
    )


def on_device(
    dp,
    mp,
    tokens,
    cotangent,
    random_blocks,
    query_weight,
    query_bias,
    key_weight,
    value_weight,
    value_bias,
    out_weight,
    out_bias,
    attn_gain,
    attn_shift,
    up_weight,
    up_bias,
    down_weight,
    down_bias,
    mlp_gain,
    mlp_shift,
):
    rank = lax.axis_index("dp") % PIECES
    spot = lax.axis_index("mp")
    seq, half = spot % 2, spot // 2
    odd = seq == 1
    sc = jnp.stack([rank, spot, seq, half]).astype(jnp.int32)

    attn_own = jnp.concatenate([query_weight.T, key_weight.T, value_weight.T, out_weight], 0)
    up_own = up_weight.T
    piece = lambda a: lax.dynamic_slice(a, (rank * PR, 0), (PR, D)).astype(F32)
    heads = random_blocks.shape[1]
    table_size = heads * (NB - 2) * RAND
    small = jnp.concatenate(
        [
            query_bias.astype(F32),
            value_bias.astype(F32),
            up_bias.astype(F32),
            random_blocks.astype(F32).reshape(-1),
        ]
    )
    small = jnp.pad(small, (0, 12 * 128 - small.shape[0])).reshape(12, 128)
    small_others = gather_line(small, mp)
    small_all = jnp.zeros((4, 12 * 128), F32)
    small_all = lax.dynamic_update_slice(small_all, small.reshape(1, -1), (spot, 0))
    for t in range(3):
        small_all = lax.dynamic_update_slice(
            small_all, small_others[t].reshape(1, -1), (spot ^ (t + 1), 0)
        )
    head_cols = D // 4
    qb = small_all[:, :head_cols].reshape(1, D)
    vb = small_all[:, head_cols : 2 * head_cols].reshape(1, D)
    ub = small_all[:, 2 * head_cols : 2 * head_cols + D].reshape(1, 4 * D)
    ub = jnp.broadcast_to(ub, (8, 4 * D))
    tables = small_all[:, 2 * head_cols + D :][:, : 2 * table_size].reshape(4, 2, table_size)
    table = jnp.where(odd, tables[:, 1], tables[:, 0]).reshape(-1).astype(jnp.int32)

    attn_pieces = gather_plane(gather_line(piece(attn_own), mp), dp)
    up_pieces = gather_plane(gather_line(piece(up_own), mp), dp)
    down_pieces = gather_plane(gather_line(piece(down_weight), mp), dp)

    w4 = call_place(
        place_attn, sc, (attn_own,) + attn_pieces, jax.ShapeDtypeStruct((4, D, D), BF16)
    )
    q, k, v, att, lse = call_attn_fwd(sc, table, tokens, w4, qb, vb)
    ffs = jax.ShapeDtypeStruct((4 * D, D), BF16)
    up, down = call_place(
        place_mlp, sc, (up_own, down_weight) + up_pieces + down_pieces, (ffs, ffs)
    )
    vecs = jnp.stack(
        [a.astype(F32) for a in (out_bias, attn_gain, attn_shift, down_bias, mlp_gain, mlp_shift)]
        + [jnp.zeros((D,), F32)] * 2
    )
    lay_own, lay_all, act, gup, hid, gml, gai, gal, gatt, sums, usum = call_middle(
        sc, att, tokens, cotangent, w4, up, down, vecs, ub
    )
    layer_out = call_put(sc, swap(lay_own, "mp", mp, 1), lay_all)

    keep, send = call_weights_mid(sc, act, gml, att, gal, hid, gup)
    mid = reduce_plane(keep, send, dp)
    low = jnp.concatenate([mid[:PR], mid[2 * PR : 3 * PR], mid[4 * PR : 4 * PR + PR // 4]], 0)
    high = jnp.concatenate([mid[PR : 2 * PR], mid[3 * PR : 4 * PR], mid[4 * PR + PR // 4 :]], 0)
    mid = pair_sum(low, high, odd, mp)
    wide = jax.ShapeDtypeStruct((D, D), F32)
    grad_down, grad_up, grad_out = call_place(
        place_mid,
        sc,
        spread_plane(mid, dp),
        (wide, wide, jax.ShapeDtypeStruct((D // 4, D), F32)),
    )
    sums_a = all_sum(jnp.concatenate([sums[:6], usum[0].reshape(2, D)], 0), dp, mp)

    dq, dk, dv, sums_b = call_attn_back(sc, table, q, k, v, gatt, lse)
    grad_own, grad_all = call_final(sc, gai, dq, dk, dv, w4)
    tokens_grad = call_put(sc, swap(grad_own, "mp", mp, 1), grad_all)
    keep_b, send_b = call_weights_qkv(sc, tokens, dq, dk, dv)
    qkv = reduce_plane(keep_b, send_b, dp)
    halves = qkv.reshape(PR, 3, 2, D // 4)
    qkv = pair_sum(
        halves[:, :, 0].reshape(PR, 3 * D // 4), halves[:, :, 1].reshape(PR, 3 * D // 4), odd, mp
    )
    narrow = jax.ShapeDtypeStruct((D, D // 4), F32)
    grad_query, grad_key, grad_value = call_place(
        place_qkv, sc, spread_plane(qkv, dp), (narrow, narrow, narrow)
    )
    sums_b = all_sum(sums_b, dp, mp)
    mine = lambda vec: lax.dynamic_slice(vec, (spot * head_cols,), (head_cols,))
    grad_up_bias = jnp.where(odd, sums_a[7], sums_a[6])
    return (
        layer_out,
        tokens_grad,
        grad_query,
        mine(sums_b[0]),
        grad_key,
        grad_value,
        mine(sums_b[1]),
        grad_out,
        sums_a[5],
        sums_a[3],
        sums_a[4],
        grad_up,
        grad_up_bias,
        grad_down,
        sums_a[2],
        sums_a[0],
        sums_a[1],
    )


def solution(mesh):
    split, rows, cols, part, copied = P("dp", None), P("mp", None), P(None, "mp"), P("mp"), P()
    return jax.shard_map(
        functools.partial(on_device, mesh.shape["dp"], mesh.shape["mp"]),
        mesh=mesh,
        in_specs=(
            split, split, P("dp", "mp", None, None),
            cols, part, cols, cols, part, rows,
            copied, copied, copied,
            cols, part, rows,
            copied, copied, copied,
        ),
        out_specs=(
            split, split,
            cols, part, cols, cols, part, rows,
            copied, copied, copied,
            cols, part, rows,
            copied, copied, copied,
        ),
        check_vma=False,
    )
```
